32 devices in a mesh: rep: 2 (over y), ep: 16 (over z, x, core).
Axes of the slice: x: 2, y: 2, z: 4, core: 2. Of those that a mesh axis runs over, the one named last changes fastest.
Arguments:
- tokens: bfloat16 [512, 2048], P(('rep', 'ep')), may hold values from -6 to 6
- logits: float32 [512, 8], P(('rep', 'ep')), may hold values from -6 to 6
- expert_ids: int32 [512, 8], P(('rep', 'ep')), may hold values from 0 to 15, all different within a row; in each aligned block of 16 rows (0 to 15, 16 to 31, ...) at most 16 rows name the same one
- w_gate_up: bfloat16 [16, 2, 2048, 1536], P('ep', None, None, 'rep'), may hold values from -0.125 to 0.125
- w_down: bfloat16 [16, 1536, 2048], P('ep', None, 'rep'), may hold values from -0.15625 to 0.15625
Outputs:
- mixed: bfloat16 [512, 2048], P(('rep', 'ep'))
The draws below stay inside these ranges and needn't reach their ends.
Inputs may be any that keep to these rules, and one draw needn't show every extreme that they name: `expert_ids`: each token names 8 different experts; the 16 tokens of one device name any one expert at most 16 times.
All inputs are finite; a program needn't handle non-finite values.
Results may differ from the reference program's by a relative error of at most 0.0057.
Values may be sent and summed in bfloat16 or wider, within the bound.
A program may use at most 64 MiB of HBM per device.

```python
import math
import jax
import jax.numpy as jnp
import numpy as np
from jax import lax

D = 2048
H = 1536
TOPK = 8
TOK_DEV = 16
E = 16
MOST = 16
TOKENS = 512
N_REP = 2
N_EP = 16


def steps_of(own_key, extent, cuts, least, top_value):
    loudness = 1.0
    for dim, blocks in cuts:
        draws = jax.random.uniform(jax.random.fold_in(jax.random.fold_in(own_key, 6), dim), (blocks,), jnp.float32, least / len(cuts), top_value / len(cuts))
        loudness = loudness * jnp.repeat(jnp.exp(draws), extent[dim] // blocks).reshape((-1,) + (1,) * (len(extent) - 1 - dim))
    return loudness


def deal_out(stream_key, own, number, rows, amount, top, limit, lean):
    ranking = jax.random.permutation(stream_key, amount)
    heavy_load, ordinary = load_shares(amount, rows * top, limit, lean, True), load_shares(amount, rows * top, limit, lean, False)
    places = jnp.arange(amount)

    def named(sizes, turn):
        used = int((sizes > 0).sum())
        fixed = max(1, used // 4)
        passed = fixed + (places - fixed + turn * (used - fixed)) % max(1, amount - fixed)
        return jnp.zeros((amount,), jnp.int32).at[ranking[jnp.where(places < fixed, places, passed)]].set(jnp.asarray(sizes, jnp.int32))

    sizes = jnp.where(number % 4 == 0, named(heavy_load, number // 4), named(ordinary, number - number // 4 - 1))
    mixed = jax.random.permutation(jax.random.fold_in(own, 3), amount)
    giver, receiver = mixed[0:amount // 2 * 2:2], mixed[1:amount // 2 * 2:2]
    room = jnp.minimum(sizes[giver] - 1, limit - sizes[receiver]) // 2
    room = jnp.where((giver == ranking[0]) | (receiver == ranking[0]) | (sizes[receiver] == 0), 0, jnp.maximum(room, 0))
    passed = jax.random.randint(jax.random.fold_in(own, 4), (amount // 2,), 0, 1 << 20) % (room + 1)
    sizes = sizes.at[giver].add(-passed).at[receiver].add(passed)
    items = jnp.searchsorted(jnp.cumsum(sizes), jnp.arange(rows * top), side="right").astype(jnp.int32)
    listing = items.reshape(top, rows).T
    listing = listing[jax.random.permutation(jax.random.fold_in(own, 1), rows)]
    turn = jax.random.randint(jax.random.fold_in(own, 2), (rows, 1), 0, top)
    return jnp.take_along_axis(listing, (jnp.arange(top)[None, :] + turn) % top, axis=1)


def load_shares(number_of, total, most, skew, full):
    portions = [(1 << 20) // math.isqrt(standing ** skew) + 1 for standing in range(1, number_of + 1)]
    largest = most if full else min(most, max(-(-total // number_of), total * portions[0] // sum(portions)))
    least = 1 if total - largest >= number_of - 1 else 0
    given, rest = [largest] + [least] * (number_of - 1), total - largest - least * (number_of - 1)
    while rest > 0:
        candidates = [i for i in range(1, number_of) if given[i] < largest] or [i for i in range(1, number_of) if given[i] < most]
        mass, remaining = sum([portions[i] for i in candidates]), rest
        for i in candidates:
            extra = min(most - given[i], max(1, remaining * portions[i] // mass), rest)
            given[i] = given[i] + extra
            rest = rest - extra
    return np.array(given)


def centred(stream_key, extent, deviation, limit, shards=(), kind=jnp.bfloat16):
    drawn = deviation * jax.random.normal(stream_key, extent, jnp.float32)
    if shards:
        drawn = drawn * steps_of(stream_key, extent, shards, -0.22, 0.18)
    return jnp.clip(drawn, -limit, limit).astype(kind)


def setup_inputs(seed: int = 0) -> dict:
    keys = jax.random.split(jax.random.key(seed), 6)
    tokens = centred(keys[0], (TOKENS, D), 1.0, 6.0, ((0, 32),))
    logits = centred(keys[1], (TOKENS, TOPK), 1.5, 6.0, ((0, 32),), jnp.float32)
    expert_ids_keys = jax.random.split(jax.random.fold_in(keys[2], 1), TOKENS // TOK_DEV)
    expert_ids_turns = jax.random.permutation(jax.random.fold_in(keys[2], 3), TOKENS // TOK_DEV)
    expert_ids = jax.vmap(lambda own, number: deal_out(jax.random.fold_in(keys[2], 2), own, number, TOK_DEV, E, TOPK, MOST, 2))(expert_ids_keys, expert_ids_turns).reshape((TOKENS, TOPK))
    w_gate_up = centred(keys[3], (E, 2, D, H), D ** -0.5, 0.125, ((0, 16), (3, 2)))
    w_down = centred(keys[4], (E, H, D), H ** -0.5, 0.15625, ((0, 16), (2, 2)))
    return dict(tokens=tokens, logits=logits, expert_ids=expert_ids, w_gate_up=w_gate_up, w_down=w_down)


def reference(tokens, logits, expert_ids, w_gate_up, w_down):
    slot_total = TOKENS * TOPK
    block_size = N_REP * N_EP * MOST
    flat_ids = expert_ids.reshape(slot_total).astype(jnp.int32)
    ordering = jnp.argsort(flat_ids, stable=True).astype(jnp.int32)
    experts = jnp.arange(E, dtype=jnp.int32)
    counts = jnp.sum((flat_ids[None, :] == experts[:, None]).astype(jnp.int32), axis=1).astype(jnp.int32)
    starts = (jnp.cumsum(counts) - counts).astype(jnp.int32)
    padded = jnp.concatenate([ordering, jnp.full((block_size,), slot_total, jnp.int32)])

    def expert_rows(triple):
        expert, start, count = triple
        picked = lax.dynamic_slice_in_dim(padded, start, block_size)
        usable = jnp.arange(block_size, dtype=jnp.int32) < count
        source = jnp.minimum(picked, slot_total - 1) // TOPK
        slot_rows = tokens[source].astype(jnp.float32)
        gate_part = jnp.dot(slot_rows, w_gate_up[expert, 0].astype(jnp.float32))
        upper = jnp.dot(slot_rows, w_gate_up[expert, 1].astype(jnp.float32))
        hidden = (jax.nn.silu(gate_part) * upper).astype(jnp.bfloat16)
        output = jnp.dot(hidden.astype(jnp.float32), w_down[expert].astype(jnp.float32)).astype(jnp.bfloat16)
        targets = jnp.where(usable, picked, slot_total).astype(jnp.int32)
        return output, targets

    outputs, targets = lax.map(expert_rows, (experts, starts, counts))
    gathered = jnp.zeros((slot_total + 1, D), jnp.bfloat16).at[targets.reshape(-1)].set(outputs.reshape(-1, D))
    per_slot = gathered[:slot_total].reshape(TOKENS, TOPK, D).astype(jnp.float32)
    scaled = jnp.exp(logits)
    weights = scaled / jnp.sum(scaled, axis=1, keepdims=True)
    mixed = jnp.sum(weights[:, :, None] * per_slot, axis=1)
    return mixed.astype(jnp.bfloat16)
```

```python
import functools

import jax
import jax.numpy as jnp
from jax import lax
from jax.experimental import pallas as pl
from jax.experimental.pallas import tpu as pltpu
from jax.sharding import PartitionSpec as P


def slot_plan(choice_ids, expert_count, capacity):
    queue_len, picks = choice_ids.shape
    flat_ids = choice_ids.reshape(queue_len * picks)
    position = jnp.arange(queue_len * picks, dtype=jnp.int32)
    earlier = (flat_ids[:, None] == flat_ids[None, :]) & (position[None, :] < position[:, None])
    slot_rank = jnp.sum(earlier.astype(jnp.int32), axis=1)
    target = flat_ids * capacity + slot_rank
    columns = jnp.arange(expert_count * capacity, dtype=jnp.int32)
    onehot = target[:, None] == columns[None, :]
    return onehot.reshape(queue_len, picks, expert_count * capacity)


def dispatch_rows(onehot, tokens):
    placing = jnp.sum(onehot.astype(jnp.bfloat16), axis=1)
    return jnp.dot(placing.T, tokens, preferred_element_type=jnp.float32).astype(jnp.bfloat16)


def to_owners(outgoing):
    return lax.all_to_all(outgoing, "ep", split_axis=0, concat_axis=0, tiled=True)


def to_sources(results):
    return lax.all_to_all(results, "ep", split_axis=0, concat_axis=0, tiled=True)


def full_units(quarter):
    return lax.all_gather(quarter, "rep", axis=1, tiled=True)


MESH = pl.DeviceIdType.MESH
PAD = 128


def dense_kernel(nz, tok_ref, logit_ref, ids_ref, wgu_ref, wd_ref, out_ref,
                 rows, gate_w, up_w, down_w, hid, own, core_in, part, z_in, pair, x_in, cross, y_in,
                 w_sem, ag_send, ag_recv, hid_send, hid_recv, core_send, core_recv,
                 z_send, z_recv, x_send, x_recv, y_send, y_recv):
    y = lax.axis_index("rep")
    ep = lax.axis_index("ep")
    z, x, c = ep // 4, (ep // 2) % 2, ep % 2
    oy, ox, oc = 1 - y, 1 - x, 1 - c
    q, width = tok_ref.shape
    units = gate_w.shape[1]
    cols = down_w.shape[1]
    half = 2 * nz * q
    full = 2 * half

    def at(yy, zz, xx, cc):
        return (yy, zz * 4 + xx * 2 + cc)

    weights = [
        pltpu.make_async_copy(wgu_ref.at[0, 0], gate_w, w_sem.at[0]),
        pltpu.make_async_copy(wgu_ref.at[0, 1], up_w, w_sem.at[1]),
        pltpu.make_async_copy(wd_ref.at[0], down_w, w_sem.at[2]),
    ]
    for w in weights:
        w.start()

    barrier = pltpu.get_barrier_semaphore()
    peers = [at(oy, z, x, c), at(y, z, ox, c), at(y, z, x, oc)]
    peers += [at(y, (z + d) % nz, x, c) for d in range(1, nz)]
    for p in peers:
        pl.semaphore_signal(barrier, inc=1, device_id=p, device_id_type=MESH)

    scaled = jnp.exp(logit_ref[...])
    soft = scaled / jnp.sum(scaled, axis=1, keepdims=True)
    lane = lax.broadcasted_iota(jnp.int32, (q, PAD), 1)
    n_ep = 4 * nz
    expert, piece = lane % n_ep, lane // n_ep
    ids = ids_ref[...]
    comb = jnp.zeros((q, PAD), jnp.float32)
    for k in range(ids.shape[1]):
        comb = comb + jnp.where(ids[:, k:k + 1] == expert, soft[:, k:k + 1], 0.0)
    hi = comb.astype(jnp.bfloat16).astype(jnp.float32)
    rest = comb - hi
    mid = rest.astype(jnp.bfloat16).astype(jnp.float32)
    low = rest - mid
    coded = jnp.where(piece == 0, hi, jnp.where(piece == 1, mid, jnp.where(piece == 2, low, 0.0)))
    rows[x, c, z, y, :, :width] = tok_ref[...]
    rows[x, c, z, y, :, width:] = coded.astype(jnp.bfloat16)
    pl.semaphore_wait(barrier, len(peers))

    sent = []

    def flat(s):
        return ((s[0] * 2 + s[1]) * nz + s[2]) * 2 + s[3]

    def ag_copy(kind, s, dev):
        return pltpu.make_async_remote_copy(
            src_ref=rows.at[s[0], s[1], s[2], s[3]], dst_ref=rows.at[s[0], s[1], s[2], s[3]],
            send_sem=ag_send.at[kind, flat(s)], recv_sem=ag_recv.at[flat(s)],
            device_id=dev, device_id_type=MESH)

    def send(kind, s, dev, cond=None):
        def go():
            ag_copy(kind, s, dev).start()
        if cond is None:
            go()
        else:
            pl.when(cond)(go)
        sent.append((kind, s, dev, cond))

    def arrive(s):
        ag_copy(0, s, peers[0]).wait_recv()

    up, down = at(y, jnp.minimum(z + 1, nz - 1), x, c), at(y, jnp.maximum(z - 1, 0), x, c)
    mine = (x, c, z, y)
    send(0, mine, peers[0])
    send(1, mine, up, z < nz - 1)
    send(2, mine, down, z > 0)
    send(3, mine, peers[1])
    send(4, mine, peers[2])
    other = (x, c, z, oy)
    arrive(other)
    send(1, other, up, z < nz - 1)
    send(2, other, down, z > 0)
    send(3, other, peers[1])
    send(4, other, peers[2])
    for d in range(1, nz):
        for rr in (y, oy):
            below = (x, c, jnp.maximum(z - d, 0), rr)
            above = (x, c, jnp.minimum(z + d, nz - 1), rr)
            has_below, has_above = z >= d, z + d <= nz - 1

            @pl.when(has_below)
            def _():
                arrive(below)
            send(1, below, up, jnp.logical_and(has_below, z < nz - 1))
            send(3, below, peers[1], has_below)
            send(4, below, peers[2], has_below)

            @pl.when(has_above)
            def _():
                arrive(above)
            send(2, above, down, jnp.logical_and(has_above, z > 0))
            send(3, above, peers[1], has_above)
            send(4, above, peers[2], has_above)

    def hid_copy(g):
        return pltpu.make_async_remote_copy(
            src_ref=hid.at[g, y], dst_ref=hid.at[g, y],
            send_sem=hid_send.at[g], recv_sem=hid_recv.at[g],
            device_id=peers[0], device_id_type=MESH)

    def hidden_of(g, xx):
        def tile(i, carry):
            at_cols = pl.ds(pl.multiple_of(i * TILE, TILE), TILE)
            block = rows[xx].reshape(full, width + PAD)[:, :width]
            gate = jnp.dot(block, gate_w[:, at_cols], preferred_element_type=jnp.float32)
            upper = jnp.dot(block, up_w[:, at_cols], preferred_element_type=jnp.float32)
            hid[g, y, :, at_cols] = (jax.nn.silu(gate) * upper).astype(jnp.bfloat16)
            return carry
        lax.fori_loop(0, units // TILE, tile, 0)
        hid_copy(g).start()

    def core_copy(g):
        return pltpu.make_async_remote_copy(
            src_ref=own.at[g, oc], dst_ref=core_in.at[g],
            send_sem=core_send.at[g], recv_sem=core_recv.at[g],
            device_id=peers[2], device_id_type=MESH)

    def z_copy(g, d):
        to = (z + d) % nz
        return pltpu.make_async_remote_copy(
            src_ref=part.at[g, to], dst_ref=z_in.at[g, d - 1],
            send_sem=z_send.at[g, d - 1], recv_sem=z_recv.at[g, d - 1],
            device_id=at(y, to, x, c), device_id_type=MESH)

    def outputs_of(g, xx):
        hid_copy(g).wait_recv()
        picked = lax.broadcasted_iota(jnp.int32, (full, PAD), 1)
        keep = jnp.logical_and(picked % n_ep == ep, picked < 3 * n_ep)
        codes = rows[xx].reshape(full, width + PAD)[:, width:].astype(jnp.float32)
        weight = jnp.sum(jnp.where(keep, codes, 0.0), axis=1, keepdims=True)

        def tile(i, carry):
            at_cols = pl.ds(pl.multiple_of(i * TILE, TILE), TILE)
            total = jnp.dot(hid[g, 0], down_w[:units, at_cols], preferred_element_type=jnp.float32)
            total += jnp.dot(hid[g, 1], down_w[units:, at_cols], preferred_element_type=jnp.float32)
            value = total.astype(jnp.bfloat16).astype(jnp.float32) * weight
            own[g, :, :, at_cols] = value.astype(jnp.bfloat16).reshape(2, half, TILE)
            return carry
        lax.fori_loop(0, cols // TILE, tile, 0)
        core_copy(g).start()

    def over_z(g):
        core_copy(g).wait_recv()
        for d in list(range(1, nz)) + [0]:
            to = (z + d) % nz
            at_rows = pl.ds(pl.multiple_of(to * 2 * q, 2 * q), 2 * q)
            total = own[g, c, at_rows, :].astype(jnp.float32) + core_in[g, at_rows, :].astype(jnp.float32)
            part[g, to] = total.astype(jnp.bfloat16)
            if d:
                z_copy(g, d).start()

    def z_total(g):
        total = part[g, z].astype(jnp.float32)
        for d in range(1, nz):
            z_copy(g, d).wait_recv()
            total = total + z_in[g, d - 1].astype(jnp.float32)
        return total

    for zz in range(nz):
        for rr in range(2):
            arrive((x, oc, zz, rr))
    for w in weights[:2]:
        w.wait()
    hidden_of(0, x)
    for zz in range(nz):
        for rr in range(2):
            s = (ox, c, zz, rr)
            arrive(s)
            send(4, s, peers[2])
    for zz in range(nz):
        for rr in range(2):
            arrive((ox, oc, zz, rr))
    hidden_of(1, ox)
    weights[2].wait()
    outputs_of(0, x)
    over_z(0)
    outputs_of(1, ox)
    over_z(1)

    x_copy = pltpu.make_async_remote_copy(
        src_ref=pair, dst_ref=x_in, send_sem=x_send, recv_sem=x_recv,
        device_id=peers[1], device_id_type=MESH)
    y_copy = pltpu.make_async_remote_copy(
        src_ref=cross.at[oy], dst_ref=y_in, send_sem=y_send, recv_sem=y_recv,
        device_id=peers[0], device_id_type=MESH)
    near = z_total(0)
    pair[...] = z_total(1).astype(jnp.bfloat16)
    x_copy.start()
    x_copy.wait_recv()
    final = (near + x_in[...].astype(jnp.float32)).astype(jnp.bfloat16)
    cross[...] = final.reshape(2, q, cols)
    y_copy.start()
    out_ref[:, pl.ds(pl.multiple_of(y * cols, cols), cols)] = cross[y]
    y_copy.wait_recv()
    out_ref[:, pl.ds(pl.multiple_of(oy * cols, cols), cols)] = y_in[...]

    for kind, s, dev, cond in sent:
        def done(kind=kind, s=s, dev=dev):
            ag_copy(kind, s, dev).wait_send()
        if cond is None:
            done()
        else:
            pl.when(cond)(done)
    for g in range(2):
        hid_copy(g).wait_send()
        core_copy(g).wait_send()
        for d in range(1, nz):
            z_copy(g, d).wait_send()
    x_copy.wait_send()
    y_copy.wait_send()


TILE = 256


def dense_body(tokens, logits, expert_ids, w_gate_up, w_down):
    nz = lax.axis_size("ep") // 4
    q, width = tokens.shape
    units = w_gate_up.shape[3]
    cols = w_down.shape[2]
    half = 2 * nz * q
    bf, sem = jnp.bfloat16, pltpu.SemaphoreType.DMA
    vmem = pl.BlockSpec(memory_space=pltpu.VMEM)
    hbm = pl.BlockSpec(memory_space=pl.ANY)
    return pl.pallas_call(
        functools.partial(dense_kernel, nz),
        out_shape=jax.ShapeDtypeStruct((q, width), bf),
        in_specs=[vmem, vmem, vmem, hbm, hbm],
        out_specs=vmem,
        scratch_shapes=[
            pltpu.VMEM((2, 2, nz, 2, q, width + PAD), bf),
            pltpu.VMEM((width, units), bf),
            pltpu.VMEM((width, units), bf),
            pltpu.VMEM((2 * units, cols), bf),
            pltpu.VMEM((2, 2, 2 * half, units), bf),
            pltpu.VMEM((2, 2, half, cols), bf),
            pltpu.VMEM((2, half, cols), bf),
            pltpu.VMEM((2, nz, 2 * q, cols), bf),
            pltpu.VMEM((2, nz - 1, 2 * q, cols), bf),
            pltpu.VMEM((2 * q, cols), bf),
            pltpu.VMEM((2 * q, cols), bf),
            pltpu.VMEM((2, q, cols), bf),
            pltpu.VMEM((q, cols), bf),
            sem((3,)),
            sem((5, 8 * nz)), sem((8 * nz,)),
            sem((2,)), sem((2,)),
            sem((2,)), sem((2,)),
            sem((2, nz - 1)), sem((2, nz - 1)),
            sem, sem, sem, sem,
        ],
        compiler_params=pltpu.CompilerParams(
            collective_id=0, has_side_effects=True, vmem_limit_bytes=48 * 1024 * 1024
        ),
    )(tokens, logits, expert_ids, w_gate_up, w_down)


def body(tokens, logits, expert_ids, w_gate_up, w_down):
    expert_count = lax.axis_size("ep")
    queue_len, picks = expert_ids.shape
    features = tokens.shape[1]
    capacity = max(2, min(queue_len, 2 * queue_len * picks // expert_count))
    if capacity == queue_len and lax.axis_size("rep") == 2 and expert_count % 8 == 0 and 3 * expert_count <= PAD:
        return dense_body(tokens, logits, expert_ids, w_gate_up, w_down)
    slot_total = expert_count * capacity
    onehot = slot_plan(expert_ids, expert_count, capacity)
    scaled = jnp.exp(logits)
    weights = scaled / jnp.sum(scaled, axis=1, keepdims=True)
    combine = jnp.sum(weights[:, :, None] * onehot.astype(jnp.float32), axis=1)
    gate_weight = w_gate_up[0, 0]
    up_weight = w_gate_up[0, 1]
    down_weight = w_down[0]
    received = to_owners(dispatch_rows(onehot, tokens).reshape(expert_count, capacity, features))
    slot_rows = received.reshape(slot_total, features)
    portion = lax.all_gather(slot_rows, "rep", axis=0, tiled=True)
    gate_part = jnp.dot(portion, gate_weight, preferred_element_type=jnp.float32)
    upper = jnp.dot(portion, up_weight, preferred_element_type=jnp.float32)
    quarter = (jax.nn.silu(gate_part) * upper).astype(jnp.bfloat16)
    hidden = full_units(quarter)
    partial_out = jnp.dot(hidden, down_weight, preferred_element_type=jnp.float32).astype(
        jnp.bfloat16
    )
    own_rows = lax.all_to_all(partial_out, "rep", split_axis=0, concat_axis=1, tiled=True)
    returned = to_sources(own_rows.reshape(expert_count, capacity, features))
    values = returned.reshape(slot_total, features)
    mixed = jnp.dot(combine, values.astype(jnp.float32), precision=lax.Precision.HIGHEST)
    return mixed.astype(jnp.bfloat16)


def solution(mesh):
    in_specs = (
        P(("rep", "ep"), None),
        P(("rep", "ep"), None),
        P(("rep", "ep"), None),
        P("ep", None, None, "rep"),
        P("ep", None, "rep"),
    )
    out_specs = P(("rep", "ep"), None)
    return jax.shard_map(body, mesh=mesh, in_specs=in_specs, out_specs=out_specs, check_vma=False)
```

```python
import functools

import jax
import jax.numpy as jnp
from jax import lax
from jax.experimental import pallas as pl
from jax.experimental.pallas import tpu as pltpu
from jax.sharding import PartitionSpec as P


def slot_plan(choice_ids, expert_count, capacity):
    queue_len, picks = choice_ids.shape
    flat_ids = choice_ids.reshape(queue_len * picks)
    position = jnp.arange(queue_len * picks, dtype=jnp.int32)
    earlier = (flat_ids[:, None] == flat_ids[None, :]) & (position[None, :] < position[:, None])
    slot_rank = jnp.sum(earlier.astype(jnp.int32), axis=1)
    target = flat_ids * capacity + slot_rank
    columns = jnp.arange(expert_count * capacity, dtype=jnp.int32)
    onehot = target[:, None] == columns[None, :]
    return onehot.reshape(queue_len, picks, expert_count * capacity)


def dispatch_rows(onehot, tokens):
    placing = jnp.sum(onehot.astype(jnp.bfloat16), axis=1)
    return jnp.dot(placing.T, tokens, preferred_element_type=jnp.float32).astype(jnp.bfloat16)


def to_owners(outgoing):
    return lax.all_to_all(outgoing, "ep", split_axis=0, concat_axis=0, tiled=True)


def to_sources(results):
    return lax.all_to_all(results, "ep", split_axis=0, concat_axis=0, tiled=True)


def full_units(quarter):
    return lax.all_gather(quarter, "rep", axis=1, tiled=True)


MESH = pl.DeviceIdType.MESH
PAD = 128


def dense_kernel(nz, tok_ref, logit_ref, ids_ref, wgu_ref, wd_ref, out_ref,
                 rows, logit_v, ids_v, gate_w, up_w, down_w, hid, own, core_in, pair, keep, x_in,
                 part, z_in, cross, y_in,
                 w_sem, ag_send, ag_recv, hid_send, hid_recv, core_send, core_recv,
                 x_send, x_recv, z_send, z_recv, y_send, y_recv):
    y = lax.axis_index("rep")
    ep = lax.axis_index("ep")
    z, x, c = ep // 4, (ep // 2) % 2, ep % 2
    oy, ox, oc = 1 - y, 1 - x, 1 - c
    q, width = tok_ref.shape
    units = gate_w.shape[1]
    cols = down_w.shape[1]
    chunk = 8 * q
    n_ep = 4 * nz

    def at(yy, zz, xx, cc):
        return (yy, zz * 4 + xx * 2 + cc)

    small = [
        pltpu.make_async_copy(logit_ref, logit_v, w_sem.at[3]),
        pltpu.make_async_copy(ids_ref, ids_v, w_sem.at[4]),
        pltpu.make_async_copy(tok_ref, rows.at[z, x, c, y, :, pl.ds(0, width)], w_sem.at[5]),
    ]
    weights = [
        pltpu.make_async_copy(wgu_ref.at[0, 0], gate_w, w_sem.at[0]),
        pltpu.make_async_copy(wgu_ref.at[0, 1], up_w, w_sem.at[1]),
        pltpu.make_async_copy(wd_ref.at[0], down_w, w_sem.at[2]),
    ]
    for w in small + weights:
        w.start()

    barrier = pltpu.get_barrier_semaphore()
    peers = [at(oy, z, x, c), at(y, z, ox, c), at(y, z, x, oc)]
    peers += [at(y, (z + d) % nz, x, c) for d in range(1, nz)]
    for p in peers:
        pl.semaphore_signal(barrier, inc=1, device_id=p, device_id_type=MESH)

    for w in small:
        w.wait()
    scaled = jnp.exp(logit_v[...])
    soft = scaled / jnp.sum(scaled, axis=0, keepdims=True)
    line = lax.broadcasted_iota(jnp.int32, (PAD, q), 0)
    expert, piece = line % n_ep, line // n_ep
    ids = ids_v[...]
    comb = jnp.zeros((PAD, q), jnp.float32)
    for k in range(ids.shape[0]):
        comb = comb + jnp.where(ids[k:k + 1, :] == expert, soft[k:k + 1, :], 0.0)
    hi = comb.astype(jnp.bfloat16).astype(jnp.float32)
    rest = comb - hi
    mid = rest.astype(jnp.bfloat16).astype(jnp.float32)
    low = rest - mid
    coded = jnp.where(piece == 0, hi, jnp.where(piece == 1, mid, jnp.where(piece == 2, low, 0.0)))
    rows[z, x, c, y, :, width:] = coded.T.astype(jnp.bfloat16)
    pl.semaphore_wait(barrier, len(peers))

    sent = []

    def ag_copy(kind, s, dev):
        flat = ((s[0] * 2 + s[1]) * 2 + s[2]) * 2 + s[3]
        return pltpu.make_async_remote_copy(
            src_ref=rows.at[s[0], s[1], s[2], s[3]], dst_ref=rows.at[s[0], s[1], s[2], s[3]],
            send_sem=ag_send.at[kind, flat], recv_sem=ag_recv.at[flat],
            device_id=dev, device_id_type=MESH)

    def send(kind, s, dev, cond=None):
        def go():
            ag_copy(kind, s, dev).start()
        if cond is None:
            go()
        else:
            pl.when(cond)(go)
        sent.append((kind, s, dev, cond))

    def arrive(s):
        ag_copy(0, s, peers[0]).wait_recv()

    near = jnp.minimum(z, nz - 1 - z)
    rising = z < nz - 1 - z
    order = [z]
    for k in range(1, nz):
        d = jnp.where(k <= 2 * near, (k + 1) // 2, k - near)
        sign = jnp.where(k <= 2 * near, -1 if k % 2 else 1, jnp.where(rising, 1, -1))
        order.append(z + sign * d)
    up, down = at(y, jnp.minimum(z + 1, nz - 1), x, c), at(y, jnp.maximum(z - 1, 0), x, c)

    def spread(s, go_up, go_down):
        send(1, s, up, go_up)
        send(2, s, down, go_down)
        send(3, s, peers[1])
        send(4, s, peers[2])

    def along_z(k):
        for rr in (y, oy):
            s = (order[k], x, c, rr)
            arrive(s)
            spread(s, jnp.logical_and(order[k] < z, z < nz - 1), jnp.logical_and(order[k] > z, z > 0))

    def along_x(k):
        for rr in (y, oy):
            s = (order[k], ox, c, rr)
            arrive(s)
            send(4, s, peers[2])

    def hid_copy(k):
        return pltpu.make_async_remote_copy(
            src_ref=hid.at[k, y], dst_ref=hid.at[k, y],
            send_sem=hid_send.at[k], recv_sem=hid_recv.at[k],
            device_id=peers[0], device_id_type=MESH)

    def hidden_of(k):
        for xx in (x, ox):
            for rr in (y, oy):
                arrive((order[k], xx, oc, rr))

        def tile(i, carry):
            at_cols = pl.ds(pl.multiple_of(i * TILE, TILE), TILE)
            block = rows[order[k]].reshape(chunk, width + PAD)[:, :width]
            gate = jnp.dot(block, gate_w[:, at_cols], preferred_element_type=jnp.float32)
            upper = jnp.dot(block, up_w[:, at_cols], preferred_element_type=jnp.float32)
            hid[k, y, :, at_cols] = (jax.nn.silu(gate) * upper).astype(jnp.bfloat16)
            return carry
        lax.fori_loop(0, units // TILE, tile, 0)
        hid_copy(k).start()

    def core_copy(k):
        return pltpu.make_async_remote_copy(
            src_ref=own.at[k, oc], dst_ref=core_in.at[k],
            send_sem=core_send.at[k], recv_sem=core_recv.at[k],
            device_id=peers[2], device_id_type=MESH)

    def x_copy(k):
        return pltpu.make_async_remote_copy(
            src_ref=pair.at[k], dst_ref=x_in.at[k],
            send_sem=x_send.at[k], recv_sem=x_recv.at[k],
            device_id=peers[1], device_id_type=MESH)

    def z_copy(k, slot):
        return pltpu.make_async_remote_copy(
            src_ref=part.at[k], dst_ref=z_in.at[slot],
            send_sem=z_send.at[k], recv_sem=z_recv.at[slot],
            device_id=at(y, order[k], x, c), device_id_type=MESH)

    def outputs_of(k):
        picked = lax.broadcasted_iota(jnp.int32, (chunk, PAD), 1)
        take = jnp.logical_and(picked % n_ep == ep, picked < 3 * n_ep)
        codes = rows[order[k]].reshape(chunk, width + PAD)[:, width:].astype(jnp.float32)
        weight = jnp.sum(jnp.where(take, codes, 0.0), axis=1, keepdims=True)
        hid_copy(k).wait_recv()

        def tile(i, carry):
            at_cols = pl.ds(pl.multiple_of(i * TILE, TILE), TILE)
            total = jnp.dot(hid[k, 0], down_w[:units, at_cols], preferred_element_type=jnp.float32)
            total += jnp.dot(hid[k, 1], down_w[units:, at_cols], preferred_element_type=jnp.float32)
            value = (total.astype(jnp.bfloat16).astype(jnp.float32) * weight).astype(jnp.bfloat16)
            for a in range(2):
                for b in range(2):
                    own[k, b, a, :, at_cols] = value[(a * 2 + b) * 2 * q:(a * 2 + b + 1) * 2 * q]
            return carry
        lax.fori_loop(0, cols // TILE, tile, 0)
        core_copy(k).start()

    def over_core(k):
        core_copy(k).wait_recv()
        far = own[k, c, ox].astype(jnp.float32) + core_in[k, ox].astype(jnp.float32)
        pair[k] = far.astype(jnp.bfloat16)
        x_copy(k).start()
        keep[k] = own[k, c, x].astype(jnp.float32) + core_in[k, x].astype(jnp.float32)

    def over_x(k):
        x_copy(k).wait_recv()
        total = keep[k] + x_in[k].astype(jnp.float32)
        if k:
            part[k] = total.astype(jnp.bfloat16)
            z_copy(k, z).start()
        else:
            keep[k] = total

    mine, other = (z, x, c, y), (z, x, c, oy)
    send(0, mine, peers[0])
    spread(mine, z < nz - 1, z > 0)
    arrive(other)
    spread(other, z < nz - 1, z > 0)
    for k in range(nz):
        if k + 1 < nz:
            along_z(k + 1)
        along_x(k)
        if k == 0:
            for w in weights[:2]:
                w.wait()
        hidden_of(k)
    weights[2].wait()
    for k in range(nz + 2):
        if k < nz:
            outputs_of(k)
        if 0 <= k - 2:
            over_x(k - 2)
        if 0 <= k - 1 < nz:
            over_core(k - 1)

    total = keep[0]
    for k in range(1, nz):
        z_copy(k, order[k]).wait_recv()
        total = total + z_in[order[k]].astype(jnp.float32)
    cross[...] = total.astype(jnp.bfloat16).reshape(2, q, cols)
    y_copy = pltpu.make_async_remote_copy(
        src_ref=cross.at[oy], dst_ref=y_in, send_sem=y_send, recv_sem=y_recv,
        device_id=peers[0], device_id_type=MESH)
    y_copy.start()
    out_ref[:, pl.ds(pl.multiple_of(y * cols, cols), cols)] = cross[y]

    for kind, s, dev, cond in sent:
        def done(kind=kind, s=s, dev=dev):
            ag_copy(kind, s, dev).wait_send()
        if cond is None:
            done()
        else:
            pl.when(cond)(done)
    for k in range(nz):
        hid_copy(k).wait_send()
        core_copy(k).wait_send()
        x_copy(k).wait_send()
        if k:
            z_copy(k, z).wait_send()
    y_copy.wait_send()
    y_copy.wait_recv()
    out_ref[:, pl.ds(pl.multiple_of(oy * cols, cols), cols)] = y_in[...]


TILE = 256


def dense_body(tokens, logits, expert_ids, w_gate_up, w_down):
    nz = lax.axis_size("ep") // 4
    q, width = tokens.shape
    picks = logits.shape[1]
    units = w_gate_up.shape[3]
    cols = w_down.shape[2]
    bf, sem = jnp.bfloat16, pltpu.SemaphoreType.DMA
    vmem = pl.BlockSpec(memory_space=pltpu.VMEM)
    hbm = pl.BlockSpec(memory_space=pl.ANY)
    return pl.pallas_call(
        functools.partial(dense_kernel, nz),
        out_shape=jax.ShapeDtypeStruct((q, width), bf),
        in_specs=[hbm] * 5,
        out_specs=vmem,
        scratch_shapes=[
            pltpu.VMEM((nz, 2, 2, 2, q, width + PAD), bf),
            pltpu.VMEM((picks, q), jnp.float32),
            pltpu.VMEM((picks, q), jnp.int32),
            pltpu.VMEM((width, units), bf),
            pltpu.VMEM((width, units), bf),
            pltpu.VMEM((2 * units, cols), bf),
            pltpu.VMEM((nz, 2, 8 * q, units), bf),
            pltpu.VMEM((nz, 2, 2, 2 * q, cols), bf),
            pltpu.VMEM((nz, 2, 2 * q, cols), bf),
            pltpu.VMEM((nz, 2 * q, cols), bf),
            pltpu.VMEM((nz, 2 * q, cols), jnp.float32),
            pltpu.VMEM((nz, 2 * q, cols), bf),
            pltpu.VMEM((nz, 2 * q, cols), bf),
            pltpu.VMEM((nz, 2 * q, cols), bf),
            pltpu.VMEM((2, q, cols), bf),
            pltpu.VMEM((q, cols), bf),
            sem((6,)),
            sem((5, 8 * nz)), sem((8 * nz,)),
            sem((nz,)), sem((nz,)),
            sem((nz,)), sem((nz,)),
            sem((nz,)), sem((nz,)),
            sem((nz,)), sem((nz,)),
            sem, sem,
        ],
        compiler_params=pltpu.CompilerParams(
            collective_id=0, has_side_effects=True, vmem_limit_bytes=60 * 1024 * 1024
        ),
    )(tokens, logits.T, expert_ids.T, w_gate_up, w_down)


def body(tokens, logits, expert_ids, w_gate_up, w_down):
    expert_count = lax.axis_size("ep")
    queue_len, picks = expert_ids.shape
    features = tokens.shape[1]
    capacity = max(2, min(queue_len, 2 * queue_len * picks // expert_count))
    if capacity == queue_len and lax.axis_size("rep") == 2 and expert_count % 8 == 0 and 3 * expert_count <= PAD:
        return dense_body(tokens, logits, expert_ids, w_gate_up, w_down)
    slot_total = expert_count * capacity
    onehot = slot_plan(expert_ids, expert_count, capacity)
    scaled = jnp.exp(logits)
    weights = scaled / jnp.sum(scaled, axis=1, keepdims=True)
    combine = jnp.sum(weights[:, :, None] * onehot.astype(jnp.float32), axis=1)
    gate_weight = w_gate_up[0, 0]
    up_weight = w_gate_up[0, 1]
    down_weight = w_down[0]
    received = to_owners(dispatch_rows(onehot, tokens).reshape(expert_count, capacity, features))
    slot_rows = received.reshape(slot_total, features)
    portion = lax.all_gather(slot_rows, "rep", axis=0, tiled=True)
    gate_part = jnp.dot(portion, gate_weight, preferred_element_type=jnp.float32)
    upper = jnp.dot(portion, up_weight, preferred_element_type=jnp.float32)
    quarter = (jax.nn.silu(gate_part) * upper).astype(jnp.bfloat16)
    hidden = full_units(quarter)
    partial_out = jnp.dot(hidden, down_weight, preferred_element_type=jnp.float32).astype(
        jnp.bfloat16
    )
    own_rows = lax.all_to_all(partial_out, "rep", split_axis=0, concat_axis=1, tiled=True)
    returned = to_sources(own_rows.reshape(expert_count, capacity, features))
    values = returned.reshape(slot_total, features)
    mixed = jnp.dot(combine, values.astype(jnp.float32), precision=lax.Precision.HIGHEST)
    return mixed.astype(jnp.bfloat16)


def solution(mesh):
    in_specs = (
        P(("rep", "ep"), None),
        P(("rep", "ep"), None),
        P(("rep", "ep"), None),
        P("ep", None, None, "rep"),
        P("ep", None, "rep"),
    )
    out_specs = P(("rep", "ep"), None)
    return jax.shard_map(body, mesh=mesh, in_specs=in_specs, out_specs=out_specs, check_vma=False)
```

```python
import functools

import jax
import jax.numpy as jnp
from jax import lax
from jax.experimental import pallas as pl
from jax.experimental.pallas import tpu as pltpu
from jax.sharding import PartitionSpec as P


def slot_plan(choice_ids, expert_count, capacity):
    queue_len, picks = choice_ids.shape
    flat_ids = choice_ids.reshape(queue_len * picks)
    position = jnp.arange(queue_len * picks, dtype=jnp.int32)
    earlier = (flat_ids[:, None] == flat_ids[None, :]) & (position[None, :] < position[:, None])
    slot_rank = jnp.sum(earlier.astype(jnp.int32), axis=1)
    target = flat_ids * capacity + slot_rank
    columns = jnp.arange(expert_count * capacity, dtype=jnp.int32)
    onehot = target[:, None] == columns[None, :]
    return onehot.reshape(queue_len, picks, expert_count * capacity)


def dispatch_rows(onehot, tokens):
    placing = jnp.sum(onehot.astype(jnp.bfloat16), axis=1)
    return jnp.dot(placing.T, tokens, preferred_element_type=jnp.float32).astype(jnp.bfloat16)


def to_owners(outgoing):
    return lax.all_to_all(outgoing, "ep", split_axis=0, concat_axis=0, tiled=True)


def to_sources(results):
    return lax.all_to_all(results, "ep", split_axis=0, concat_axis=0, tiled=True)


def full_units(quarter):
    return lax.all_gather(quarter, "rep", axis=1, tiled=True)


MESH = pl.DeviceIdType.MESH
PAD = 128


def dense_kernel(nz, tok_ref, logit_ref, ids_ref, wgu_ref, wd_ref, out_ref,
                 rows, logit_v, ids_v, gate_w, up_w, down_w, hid, own, core_in, pair, keep, x_in,
                 part, z_in, cross, y_in,
                 w_sem, ag_send, ag_recv, hid_send, hid_recv, core_send, core_recv,
                 x_send, x_recv, z_send, z_recv, y_send, y_recv):
    y = lax.axis_index("rep")
    ep = lax.axis_index("ep")
    z, x, c = ep // 4, (ep // 2) % 2, ep % 2
    oy, ox, oc = 1 - y, 1 - x, 1 - c
    q, width = tok_ref.shape
    units = gate_w.shape[1]
    cols = down_w.shape[1]
    chunk = 8 * q
    n_ep = 4 * nz

    def at(yy, zz, xx, cc):
        return (yy, zz * 4 + xx * 2 + cc)

    small = [
        pltpu.make_async_copy(logit_ref, logit_v, w_sem.at[3]),
        pltpu.make_async_copy(ids_ref, ids_v, w_sem.at[4]),
        pltpu.make_async_copy(tok_ref, rows.at[z, x, c, y, :, pl.ds(0, width)], w_sem.at[5]),
    ]
    weights = [
        pltpu.make_async_copy(wgu_ref.at[0, 0], gate_w, w_sem.at[0]),
        pltpu.make_async_copy(wgu_ref.at[0, 1], up_w, w_sem.at[1]),
        pltpu.make_async_copy(wd_ref.at[0], down_w, w_sem.at[2]),
    ]
    for w in small + weights:
        w.start()

    barrier = pltpu.get_barrier_semaphore()
    peers = [at(oy, z, x, c), at(y, z, ox, c), at(y, z, x, oc)]
    peers += [at(y, (z + d) % nz, x, c) for d in range(1, nz)]
    for p in peers:
        pl.semaphore_signal(barrier, inc=1, device_id=p, device_id_type=MESH)

    for w in small:
        w.wait()
    scaled = jnp.exp(logit_v[...])
    soft = scaled / jnp.sum(scaled, axis=0, keepdims=True)
    line = lax.broadcasted_iota(jnp.int32, (PAD, q), 0)
    expert, piece = line % n_ep, line // n_ep
    ids = ids_v[...]
    comb = jnp.zeros((PAD, q), jnp.float32)
    for k in range(ids.shape[0]):
        comb = comb + jnp.where(ids[k:k + 1, :] == expert, soft[k:k + 1, :], 0.0)
    hi = comb.astype(jnp.bfloat16).astype(jnp.float32)
    rest = comb - hi
    mid = rest.astype(jnp.bfloat16).astype(jnp.float32)
    low = rest - mid
    coded = jnp.where(piece == 0, hi, jnp.where(piece == 1, mid, jnp.where(piece == 2, low, 0.0)))
    rows[z, x, c, y, :, width:] = coded.T.astype(jnp.bfloat16)
    pl.semaphore_wait(barrier, len(peers))

    sent = []

    def ag_copy(kind, s, dev):
        flat = ((s[0] * 2 + s[1]) * 2 + s[2]) * 2 + s[3]
        return pltpu.make_async_remote_copy(
            src_ref=rows.at[s[0], s[1], s[2], s[3]], dst_ref=rows.at[s[0], s[1], s[2], s[3]],
            send_sem=ag_send.at[kind, flat], recv_sem=ag_recv.at[flat],
            device_id=dev, device_id_type=MESH)

    def send(kind, s, dev, cond=None):
        def go():
            ag_copy(kind, s, dev).start()
        if cond is None:
            go()
        else:
            pl.when(cond)(go)
        sent.append((kind, s, dev, cond))

    def arrive(s):
        ag_copy(0, s, peers[0]).wait_recv()

    near = jnp.minimum(z, nz - 1 - z)
    rising = z < nz - 1 - z
    order = [z]
    for k in range(1, nz):
        d = jnp.where(k <= 2 * near, (k + 1) // 2, k - near)
        sign = jnp.where(k <= 2 * near, -1 if k % 2 else 1, jnp.where(rising, 1, -1))
        order.append(z + sign * d)
    up, down = at(y, jnp.minimum(z + 1, nz - 1), x, c), at(y, jnp.maximum(z - 1, 0), x, c)

    def spread(s, go_up, go_down):
        send(1, s, up, go_up)
        send(2, s, down, go_down)
        send(3, s, peers[1])
        send(4, s, peers[2])

    def along_z(k):
        for rr in (y, oy):
            s = (order[k], x, c, rr)
            arrive(s)
            spread(s, jnp.logical_and(order[k] < z, z < nz - 1), jnp.logical_and(order[k] > z, z > 0))

    def along_x(k):
        for rr in (y, oy):
            s = (order[k], ox, c, rr)
            arrive(s)
            send(4, s, peers[2])

    def hid_copy(k):
        return pltpu.make_async_remote_copy(
            src_ref=hid.at[k, y], dst_ref=hid.at[k, y],
            send_sem=hid_send.at[k], recv_sem=hid_recv.at[k],
            device_id=peers[0], device_id_type=MESH)

    def hidden_of(k):
        for xx in (x, ox):
            for rr in (y, oy):
                arrive((order[k], xx, oc, rr))

        def tile(i, carry):
            at_cols = pl.ds(pl.multiple_of(i * TILE, TILE), TILE)
            block = rows[order[k]].reshape(chunk, width + PAD)[:, :width]
            gate = jnp.dot(block, gate_w[:, at_cols], preferred_element_type=jnp.float32)
            upper = jnp.dot(block, up_w[:, at_cols], preferred_element_type=jnp.float32)
            hid[k, y, :, at_cols] = (jax.nn.silu(gate) * upper).astype(jnp.bfloat16)
            return carry
        lax.fori_loop(0, units // TILE, tile, 0)
        hid_copy(k).start()

    def core_copy(k):
        return pltpu.make_async_remote_copy(
            src_ref=own.at[k, oc], dst_ref=core_in.at[k],
            send_sem=core_send.at[k], recv_sem=core_recv.at[k],
            device_id=peers[2], device_id_type=MESH)

    def x_copy(k):
        return pltpu.make_async_remote_copy(
            src_ref=pair.at[k], dst_ref=x_in.at[k],
            send_sem=x_send.at[k], recv_sem=x_recv.at[k],
            device_id=peers[1], device_id_type=MESH)

    def z_copy(k, slot):
        return pltpu.make_async_remote_copy(
            src_ref=part.at[k], dst_ref=z_in.at[slot],
            send_sem=z_send.at[k], recv_sem=z_recv.at[slot],
            device_id=at(y, order[k], x, c), device_id_type=MESH)

    def outputs_of(k):
        picked = lax.broadcasted_iota(jnp.int32, (chunk, PAD), 1)
        take = jnp.logical_and(picked % n_ep == ep, picked < 3 * n_ep)
        codes = rows[order[k]].reshape(chunk, width + PAD)[:, width:].astype(jnp.float32)
        weight = jnp.sum(jnp.where(take, codes, 0.0), axis=1, keepdims=True)
        hid_copy(k).wait_recv()

        def tile(i, carry):
            at_cols = pl.ds(pl.multiple_of(i * TILE, TILE), TILE)
            total = jnp.dot(hid[k, 0], down_w[:units, at_cols], preferred_element_type=jnp.float32)
            total += jnp.dot(hid[k, 1], down_w[units:, at_cols], preferred_element_type=jnp.float32)
            value = (total.astype(jnp.bfloat16).astype(jnp.float32) * weight).astype(jnp.bfloat16)
            for a in range(2):
                for b in range(2):
                    own[k, b, a, :, at_cols] = value[(a * 2 + b) * 2 * q:(a * 2 + b + 1) * 2 * q]
            return carry
        lax.fori_loop(0, cols // TILE, tile, 0)
        core_copy(k).start()

    def over_core(k):
        core_copy(k).wait_recv()
        far = own[k, c, ox].astype(jnp.float32) + core_in[k, ox].astype(jnp.float32)
        pair[k] = far.astype(jnp.bfloat16)
        x_copy(k).start()
        keep[k] = own[k, c, x].astype(jnp.float32) + core_in[k, x].astype(jnp.float32)

    def over_x(k):
        x_copy(k).wait_recv()
        total = keep[k] + x_in[k].astype(jnp.float32)
        if k:
            part[k] = total.astype(jnp.bfloat16)
            z_copy(k, z).start()
        else:
            keep[k] = total

    mine, other = (z, x, c, y), (z, x, c, oy)
    send(0, mine, peers[0])
    spread(mine, z < nz - 1, z > 0)
    arrive(other)
    spread(other, z < nz - 1, z > 0)
    for k in range(nz):
        if k + 1 < nz:
            along_z(k + 1)
        along_x(k)
        if k == 0:
            for w in weights[:2]:
                w.wait()
        if k == nz - 1:
            if nz > 2:
                outputs_of(nz - 3)
            for j in range(max(nz - 3, 0)):
                over_core(j)
        hidden_of(k)
        if k == nz - 2:
            weights[2].wait()
            for j in range(max(nz - 3, 0)):
                outputs_of(j)
    if nz < 2:
        weights[2].wait()
    for k in range(max(nz - 4, 0)):
        over_x(k)
    for k in range(max(nz - 3, 0), nz + 1):
        if k > max(nz - 3, 0) or nz < 3:
            if k < nz:
                outputs_of(k)
        if k > 0:
            over_x(k - 1)
        if k < nz:
            over_core(k)

    total = keep[0]
    for k in range(1, nz):
        z_copy(k, order[k]).wait_recv()
        total = total + z_in[order[k]].astype(jnp.float32)
    cross[...] = total.astype(jnp.bfloat16).reshape(2, q, cols)
    y_copy = pltpu.make_async_remote_copy(
        src_ref=cross.at[oy], dst_ref=y_in, send_sem=y_send, recv_sem=y_recv,
        device_id=peers[0], device_id_type=MESH)
    y_copy.start()
    out_ref[:, pl.ds(pl.multiple_of(y * cols, cols), cols)] = cross[y]

    for kind, s, dev, cond in sent:
        def done(kind=kind, s=s, dev=dev):
            ag_copy(kind, s, dev).wait_send()
        if cond is None:
            done()
        else:
            pl.when(cond)(done)
    for k in range(nz):
        hid_copy(k).wait_send()
        core_copy(k).wait_send()
        x_copy(k).wait_send()
        if k:
            z_copy(k, z).wait_send()
    y_copy.wait_send()
    y_copy.wait_recv()
    out_ref[:, pl.ds(pl.multiple_of(oy * cols, cols), cols)] = y_in[...]


TILE = 256


def dense_body(tokens, logits, expert_ids, w_gate_up, w_down):
    nz = lax.axis_size("ep") // 4
    q, width = tokens.shape
    picks = logits.shape[1]
    units = w_gate_up.shape[3]
    cols = w_down.shape[2]
    bf, sem = jnp.bfloat16, pltpu.SemaphoreType.DMA
    vmem = pl.BlockSpec(memory_space=pltpu.VMEM)
    hbm = pl.BlockSpec(memory_space=pl.ANY)
    return pl.pallas_call(
        functools.partial(dense_kernel, nz),
        out_shape=jax.ShapeDtypeStruct((q, width), bf),
        in_specs=[hbm] * 5,
        out_specs=vmem,
        scratch_shapes=[
            pltpu.VMEM((nz, 2, 2, 2, q, width + PAD), bf),
            pltpu.VMEM((picks, q), jnp.float32),
            pltpu.VMEM((picks, q), jnp.int32),
            pltpu.VMEM((width, units), bf),
            pltpu.VMEM((width, units), bf),
            pltpu.VMEM((2 * units, cols), bf),
            pltpu.VMEM((nz, 2, 8 * q, units), bf),
            pltpu.VMEM((nz, 2, 2, 2 * q, cols), bf),
            pltpu.VMEM((nz, 2, 2 * q, cols), bf),
            pltpu.VMEM((nz, 2 * q, cols), bf),
            pltpu.VMEM((nz, 2 * q, cols), jnp.float32),
            pltpu.VMEM((nz, 2 * q, cols), bf),
            pltpu.VMEM((nz, 2 * q, cols), bf),
            pltpu.VMEM((nz, 2 * q, cols), bf),
            pltpu.VMEM((2, q, cols), bf),
            pltpu.VMEM((q, cols), bf),
            sem((6,)),
            sem((5, 8 * nz)), sem((8 * nz,)),
            sem((nz,)), sem((nz,)),
            sem((nz,)), sem((nz,)),
            sem((nz,)), sem((nz,)),
            sem((nz,)), sem((nz,)),
            sem, sem,
        ],
        compiler_params=pltpu.CompilerParams(
            collective_id=0, has_side_effects=True, vmem_limit_bytes=60 * 1024 * 1024
        ),
    )(tokens, logits.T, expert_ids.T, w_gate_up, w_down)


def body(tokens, logits, expert_ids, w_gate_up, w_down):
    expert_count = lax.axis_size("ep")
    queue_len, picks = expert_ids.shape
    features = tokens.shape[1]
    capacity = max(2, min(queue_len, 2 * queue_len * picks // expert_count))
    if capacity == queue_len and lax.axis_size("rep") == 2 and expert_count % 8 == 0 and 3 * expert_count <= PAD:
        return dense_body(tokens, logits, expert_ids, w_gate_up, w_down)
    slot_total = expert_count * capacity
    onehot = slot_plan(expert_ids, expert_count, capacity)
    scaled = jnp.exp(logits)
    weights = scaled / jnp.sum(scaled, axis=1, keepdims=True)
    combine = jnp.sum(weights[:, :, None] * onehot.astype(jnp.float32), axis=1)
    gate_weight = w_gate_up[0, 0]
    up_weight = w_gate_up[0, 1]
    down_weight = w_down[0]
    received = to_owners(dispatch_rows(onehot, tokens).reshape(expert_count, capacity, features))
    slot_rows = received.reshape(slot_total, features)
    portion = lax.all_gather(slot_rows, "rep", axis=0, tiled=True)
    gate_part = jnp.dot(portion, gate_weight, preferred_element_type=jnp.float32)
    upper = jnp.dot(portion, up_weight, preferred_element_type=jnp.float32)
    quarter = (jax.nn.silu(gate_part) * upper).astype(jnp.bfloat16)
    hidden = full_units(quarter)
    partial_out = jnp.dot(hidden, down_weight, preferred_element_type=jnp.float32).astype(
        jnp.bfloat16
    )
    own_rows = lax.all_to_all(partial_out, "rep", split_axis=0, concat_axis=1, tiled=True)
    returned = to_sources(own_rows.reshape(expert_count, capacity, features))
    values = returned.reshape(slot_total, features)
    mixed = jnp.dot(combine, values.astype(jnp.float32), precision=lax.Precision.HIGHEST)
    return mixed.astype(jnp.bfloat16)


def solution(mesh):
    in_specs = (
        P(("rep", "ep"), None),
        P(("rep", "ep"), None),
        P(("rep", "ep"), None),
        P("ep", None, None, "rep"),
        P("ep", None, "rep"),
    )
    out_specs = P(("rep", "ep"), None)
    return jax.shard_map(body, mesh=mesh, in_specs=in_specs, out_specs=out_specs, check_vma=False)
```

```python
import functools

import jax
import jax.numpy as jnp
from jax import lax
from jax.experimental import pallas as pl
from jax.experimental.pallas import tpu as pltpu
from jax.sharding import PartitionSpec as P


def slot_plan(choice_ids, expert_count, capacity):
    queue_len, picks = choice_ids.shape
    flat_ids = choice_ids.reshape(queue_len * picks)
    position = jnp.arange(queue_len * picks, dtype=jnp.int32)
    earlier = (flat_ids[:, None] == flat_ids[None, :]) & (position[None, :] < position[:, None])
    slot_rank = jnp.sum(earlier.astype(jnp.int32), axis=1)
    target = flat_ids * capacity + slot_rank
    columns = jnp.arange(expert_count * capacity, dtype=jnp.int32)
    onehot = target[:, None] == columns[None, :]
    return onehot.reshape(queue_len, picks, expert_count * capacity)


def dispatch_rows(onehot, tokens):
    placing = jnp.sum(onehot.astype(jnp.bfloat16), axis=1)
    return jnp.dot(placing.T, tokens, preferred_element_type=jnp.float32).astype(jnp.bfloat16)


def to_owners(outgoing):
    return lax.all_to_all(outgoing, "ep", split_axis=0, concat_axis=0, tiled=True)


def to_sources(results):
    return lax.all_to_all(results, "ep", split_axis=0, concat_axis=0, tiled=True)


def full_units(quarter):
    return lax.all_gather(quarter, "rep", axis=1, tiled=True)


MESH = pl.DeviceIdType.MESH
PAD = 128


def dense_kernel(nz, tok_ref, logit_ref, ids_ref, wgu_ref, wd_ref, out_ref,
                 rows, logit_v, ids_v, gate_w, up_w, down_w, hid, own, core_in, pair, keep, x_in,
                 part, z_in, cross, y_in,
                 w_sem, ag_send, ag_recv, hid_send, hid_recv, core_send, core_recv,
                 x_send, x_recv, z_send, z_recv, y_send, y_recv):
    y = lax.axis_index("rep")
    ep = lax.axis_index("ep")
    z, x, c = ep // 4, (ep // 2) % 2, ep % 2
    oy, ox, oc = 1 - y, 1 - x, 1 - c
    q, width = tok_ref.shape
    units = gate_w.shape[1]
    cols = down_w.shape[1]
    chunk = 8 * q
    n_ep = 4 * nz

    def at(yy, zz, xx, cc):
        return (yy, zz * 4 + xx * 2 + cc)

    small = [
        pltpu.make_async_copy(logit_ref, logit_v, w_sem.at[3]),
        pltpu.make_async_copy(ids_ref, ids_v, w_sem.at[4]),
        pltpu.make_async_copy(tok_ref, rows.at[z, x, c, y, :, pl.ds(0, width)], w_sem.at[5]),
    ]
    weights = [
        pltpu.make_async_copy(wgu_ref.at[0, 0], gate_w, w_sem.at[0]),
        pltpu.make_async_copy(wgu_ref.at[0, 1], up_w, w_sem.at[1]),
        pltpu.make_async_copy(wd_ref.at[0], down_w, w_sem.at[2]),
    ]
    for w in small + weights:
        w.start()

    barrier = pltpu.get_barrier_semaphore()
    peers = [at(oy, z, x, c), at(y, z, ox, c), at(y, z, x, oc)]
    peers += [at(y, (z + d) % nz, x, c) for d in range(1, nz)]
    for p in peers:
        pl.semaphore_signal(barrier, inc=1, device_id=p, device_id_type=MESH)

    for w in small:
        w.wait()
    scaled = jnp.exp(logit_v[...])
    soft = scaled / jnp.sum(scaled, axis=0, keepdims=True)
    line = lax.broadcasted_iota(jnp.int32, (PAD, q), 0)
    expert, piece = line % n_ep, line // n_ep
    ids = ids_v[...]
    comb = jnp.zeros((PAD, q), jnp.float32)
    for k in range(ids.shape[0]):
        comb = comb + jnp.where(ids[k:k + 1, :] == expert, soft[k:k + 1, :], 0.0)
    hi = comb.astype(jnp.bfloat16).astype(jnp.float32)
    rest = comb - hi
    mid = rest.astype(jnp.bfloat16).astype(jnp.float32)
    low = rest - mid
    coded = jnp.where(piece == 0, hi, jnp.where(piece == 1, mid, jnp.where(piece == 2, low, 0.0)))
    rows[z, x, c, y, :, width:] = coded.T.astype(jnp.bfloat16)
    pl.semaphore_wait(barrier, len(peers))

    sent = []

    def ag_copy(kind, s, dev):
        flat = ((s[0] * 2 + s[1]) * 2 + s[2]) * 2 + s[3]
        return pltpu.make_async_remote_copy(
            src_ref=rows.at[s[0], s[1], s[2], s[3]], dst_ref=rows.at[s[0], s[1], s[2], s[3]],
            send_sem=ag_send.at[kind, flat], recv_sem=ag_recv.at[flat],
            device_id=dev, device_id_type=MESH)

    def send(kind, s, dev, cond=None):
        def go():
            ag_copy(kind, s, dev).start()
        if cond is None:
            go()
        else:
            pl.when(cond)(go)
        sent.append((kind, s, dev, cond))

    def arrive(s):
        ag_copy(0, s, peers[0]).wait_recv()

    near = jnp.minimum(z, nz - 1 - z)
    rising = z < nz - 1 - z
    order = [z]
    for k in range(1, nz):
        d = jnp.where(k <= 2 * near, (k + 1) // 2, k - near)
        sign = jnp.where(k <= 2 * near, -1 if k % 2 else 1, jnp.where(rising, 1, -1))
        order.append(z + sign * d)
    up, down = at(y, jnp.minimum(z + 1, nz - 1), x, c), at(y, jnp.maximum(z - 1, 0), x, c)

    def spread(s, go_up, go_down):
        send(1, s, up, go_up)
        send(2, s, down, go_down)
        send(3, s, peers[1])
        send(4, s, peers[2])

    def along_z(k):
        for rr in (y, oy):
            s = (order[k], x, c, rr)
            arrive(s)
            spread(s, jnp.logical_and(order[k] < z, z < nz - 1), jnp.logical_and(order[k] > z, z > 0))

    def along_x(k):
        for rr in (y, oy):
            s = (order[k], ox, c, rr)
            arrive(s)
            send(4, s, peers[2])

    def hid_copy(k, i):
        at_cols = pl.ds(pl.multiple_of(i * TILE, TILE), TILE)
        return pltpu.make_async_remote_copy(
            src_ref=hid.at[k, y, :, at_cols], dst_ref=hid.at[k, y, :, at_cols],
            send_sem=hid_send.at[k, i], recv_sem=hid_recv.at[k, i],
            device_id=peers[0], device_id_type=MESH)

    def hidden_of(k):
        for xx in (x, ox):
            for rr in (y, oy):
                arrive((order[k], xx, oc, rr))

        def tile(i, carry):
            at_cols = pl.ds(pl.multiple_of(i * TILE, TILE), TILE)
            block = rows[order[k]].reshape(chunk, width + PAD)[:, :width]
            gate = jnp.dot(block, gate_w[:, at_cols], preferred_element_type=jnp.float32)
            upper = jnp.dot(block, up_w[:, at_cols], preferred_element_type=jnp.float32)
            hid[k, y, :, at_cols] = (jax.nn.silu(gate) * upper).astype(jnp.bfloat16)
            hid_copy(k, i).start()
            return carry
        lax.fori_loop(0, units // TILE, tile, 0)

    def core_copy(k):
        return pltpu.make_async_remote_copy(
            src_ref=own.at[k, oc], dst_ref=core_in.at[k],
            send_sem=core_send.at[k], recv_sem=core_recv.at[k],
            device_id=peers[2], device_id_type=MESH)

    def x_copy(k):
        return pltpu.make_async_remote_copy(
            src_ref=pair.at[k], dst_ref=x_in.at[k],
            send_sem=x_send.at[k], recv_sem=x_recv.at[k],
            device_id=peers[1], device_id_type=MESH)

    def z_copy(k, slot):
        return pltpu.make_async_remote_copy(
            src_ref=part.at[k], dst_ref=z_in.at[slot],
            send_sem=z_send.at[k], recv_sem=z_recv.at[slot],
            device_id=at(y, order[k], x, c), device_id_type=MESH)

    def outputs_of(k):
        picked = lax.broadcasted_iota(jnp.int32, (chunk, PAD), 1)
        take = jnp.logical_and(picked % n_ep == ep, picked < 3 * n_ep)
        codes = rows[order[k]].reshape(chunk, width + PAD)[:, width:].astype(jnp.float32)
        weight = jnp.sum(jnp.where(take, codes, 0.0), axis=1, keepdims=True)
        for i in range(units // TILE):
            hid_copy(k, i).wait_recv()

        def tile(i, carry):
            at_cols = pl.ds(pl.multiple_of(i * TILE, TILE), TILE)
            total = jnp.dot(hid[k, 0], down_w[:units, at_cols], preferred_element_type=jnp.float32)
            total += jnp.dot(hid[k, 1], down_w[units:, at_cols], preferred_element_type=jnp.float32)
            value = (total.astype(jnp.bfloat16).astype(jnp.float32) * weight).astype(jnp.bfloat16)
            for a in range(2):
                for b in range(2):
                    own[k, b, a, :, at_cols] = value[(a * 2 + b) * 2 * q:(a * 2 + b + 1) * 2 * q]
            return carry
        lax.fori_loop(0, cols // TILE, tile, 0)
        core_copy(k).start()

    def over_core(k):
        core_copy(k).wait_recv()
        far = own[k, c, ox].astype(jnp.float32) + core_in[k, ox].astype(jnp.float32)
        pair[k] = far.astype(jnp.bfloat16)
        x_copy(k).start()
        keep[k] = own[k, c, x].astype(jnp.float32) + core_in[k, x].astype(jnp.float32)

    def over_x(k):
        x_copy(k).wait_recv()
        total = keep[k] + x_in[k].astype(jnp.float32)
        if k:
            part[k] = total.astype(jnp.bfloat16)
            z_copy(k, z).start()
        else:
            keep[k] = total

    mine, other = (z, x, c, y), (z, x, c, oy)
    send(0, mine, peers[0])
    spread(mine, z < nz - 1, z > 0)
    arrive(other)
    spread(other, z < nz - 1, z > 0)
    for k in range(nz):
        if k + 1 < nz:
            along_z(k + 1)
        along_x(k)
        if k == 0:
            for w in weights[:2]:
                w.wait()
        if k == nz - 1:
            if nz > 2:
                outputs_of(nz - 3)
            for j in range(max(nz - 3, 0)):
                over_core(j)
        hidden_of(k)
        if k == nz - 2:
            weights[2].wait()
            for j in range(max(nz - 3, 0)):
                outputs_of(j)
    if nz < 2:
        weights[2].wait()
    for k in range(max(nz - 4, 0)):
        over_x(k)
    for k in range(max(nz - 3, 0), nz + 1):
        if k > max(nz - 3, 0) or nz < 3:
            if k < nz:
                outputs_of(k)
        if k > 0:
            over_x(k - 1)
        if k < nz:
            over_core(k)

    total = keep[0]
    for k in range(1, nz):
        z_copy(k, order[k]).wait_recv()
        total = total + z_in[order[k]].astype(jnp.float32)
    cross[...] = total.astype(jnp.bfloat16).reshape(2, q, cols)
    y_copy = pltpu.make_async_remote_copy(
        src_ref=cross.at[oy], dst_ref=y_in, send_sem=y_send, recv_sem=y_recv,
        device_id=peers[0], device_id_type=MESH)
    y_copy.start()
    out_ref[:, pl.ds(pl.multiple_of(y * cols, cols), cols)] = cross[y]

    for kind, s, dev, cond in sent:
        def done(kind=kind, s=s, dev=dev):
            ag_copy(kind, s, dev).wait_send()
        if cond is None:
            done()
        else:
            pl.when(cond)(done)
    for k in range(nz):
        for i in range(units // TILE):
            hid_copy(k, i).wait_send()
        core_copy(k).wait_send()
        x_copy(k).wait_send()
        if k:
            z_copy(k, z).wait_send()
    y_copy.wait_send()
    y_copy.wait_recv()
    out_ref[:, pl.ds(pl.multiple_of(oy * cols, cols), cols)] = y_in[...]


TILE = 256


def dense_body(tokens, logits, expert_ids, w_gate_up, w_down):
    nz = lax.axis_size("ep") // 4
    q, width = tokens.shape
    picks = logits.shape[1]
    units = w_gate_up.shape[3]
    cols = w_down.shape[2]
    bf, sem = jnp.bfloat16, pltpu.SemaphoreType.DMA
    vmem = pl.BlockSpec(memory_space=pltpu.VMEM)
    hbm = pl.BlockSpec(memory_space=pl.ANY)
    return pl.pallas_call(
        functools.partial(dense_kernel, nz),
        out_shape=jax.ShapeDtypeStruct((q, width), bf),
        in_specs=[hbm] * 5,
        out_specs=vmem,
        scratch_shapes=[
            pltpu.VMEM((nz, 2, 2, 2, q, width + PAD), bf),
            pltpu.VMEM((picks, q), jnp.float32),
            pltpu.VMEM((picks, q), jnp.int32),
            pltpu.VMEM((width, units), bf),
            pltpu.VMEM((width, units), bf),
            pltpu.VMEM((2 * units, cols), bf),
            pltpu.VMEM((nz, 2, 8 * q, units), bf),
            pltpu.VMEM((nz, 2, 2, 2 * q, cols), bf),
            pltpu.VMEM((nz, 2, 2 * q, cols), bf),
            pltpu.VMEM((nz, 2 * q, cols), bf),
            pltpu.VMEM((nz, 2 * q, cols), jnp.float32),
            pltpu.VMEM((nz, 2 * q, cols), bf),
            pltpu.VMEM((nz, 2 * q, cols), bf),
            pltpu.VMEM((nz, 2 * q, cols), bf),
            pltpu.VMEM((2, q, cols), bf),
            pltpu.VMEM((q, cols), bf),
            sem((6,)),
            sem((5, 8 * nz)), sem((8 * nz,)),
            sem((nz, units // TILE)), sem((nz, units // TILE)),
            sem((nz,)), sem((nz,)),
            sem((nz,)), sem((nz,)),
            sem((nz,)), sem((nz,)),
            sem, sem,
        ],
        compiler_params=pltpu.CompilerParams(
            collective_id=0, has_side_effects=True, vmem_limit_bytes=60 * 1024 * 1024
        ),
    )(tokens, logits.T, expert_ids.T, w_gate_up, w_down)


def body(tokens, logits, expert_ids, w_gate_up, w_down):
    expert_count = lax.axis_size("ep")
    queue_len, picks = expert_ids.shape
    features = tokens.shape[1]
    capacity = max(2, min(queue_len, 2 * queue_len * picks // expert_count))
    if capacity == queue_len and lax.axis_size("rep") == 2 and expert_count % 8 == 0 and 3 * expert_count <= PAD:
        return dense_body(tokens, logits, expert_ids, w_gate_up, w_down)
    slot_total = expert_count * capacity
    onehot = slot_plan(expert_ids, expert_count, capacity)
    scaled = jnp.exp(logits)
    weights = scaled / jnp.sum(scaled, axis=1, keepdims=True)
    combine = jnp.sum(weights[:, :, None] * onehot.astype(jnp.float32), axis=1)
    gate_weight = w_gate_up[0, 0]
    up_weight = w_gate_up[0, 1]
    down_weight = w_down[0]
    received = to_owners(dispatch_rows(onehot, tokens).reshape(expert_count, capacity, features))
    slot_rows = received.reshape(slot_total, features)
    portion = lax.all_gather(slot_rows, "rep", axis=0, tiled=True)
    gate_part = jnp.dot(portion, gate_weight, preferred_element_type=jnp.float32)
    upper = jnp.dot(portion, up_weight, preferred_element_type=jnp.float32)
    quarter = (jax.nn.silu(gate_part) * upper).astype(jnp.bfloat16)
    hidden = full_units(quarter)
    partial_out = jnp.dot(hidden, down_weight, preferred_element_type=jnp.float32).astype(
        jnp.bfloat16
    )
    own_rows = lax.all_to_all(partial_out, "rep", split_axis=0, concat_axis=1, tiled=True)
    returned = to_sources(own_rows.reshape(expert_count, capacity, features))
    values = returned.reshape(slot_total, features)
    mixed = jnp.dot(combine, values.astype(jnp.float32), precision=lax.Precision.HIGHEST)
    return mixed.astype(jnp.bfloat16)


def solution(mesh):
    in_specs = (
        P(("rep", "ep"), None),
        P(("rep", "ep"), None),
        P(("rep", "ep"), None),
        P("ep", None, None, "rep"),
        P("ep", None, "rep"),
    )
    out_specs = P(("rep", "ep"), None)
    return jax.shard_map(body, mesh=mesh, in_specs=in_specs, out_specs=out_specs, check_vma=False)
```
